32 devices in a mesh: grid: 32 (over z, y, x, core), freq: 1.
Axes of the slice: x: 2, y: 2, z: 4, core: 2. Of those that a mesh axis runs over, the one named last changes fastest.
Arguments:
- replicas: bfloat16 [2, 16384, 2, 512], P('freq', 'grid'), may hold values from -6 to 6
- csm: bfloat16 [2, 2, 512, 512], P('freq', None, 'grid'), as said below
- inverse: bfloat16 [2, 2, 512, 512], P('freq', None, 'grid'), as said below
Outputs:
- bartlett: float32 [16384], P(('grid', 'freq'))
- mvdr: float32 [16384], P(('grid', 'freq'))
The draws below stay inside these ranges and needn't reach their ends.
Inputs may be any that keep to these rules, and one draw needn't show every extreme that they name: csm[f, 0] + i csm[f, 1] is Hermitian positive definite for every bin. inverse[f, 0] + i inverse[f, 1] is Hermitian positive definite for every bin.
All inputs are finite; a program needn't handle non-finite values.
Results may differ from the reference program's by a relative error of at most 0.0003.
Values may be sent and summed in bfloat16 or wider, within the bound.
A program may use at most 64 MiB of HBM per device.

```python
import jax
import jax.numpy as jnp
from jax import lax

M = 512
F = 2
G = 16384


def hermitian(key):
    first, second, third, fourth = jax.random.split(key, 4)
    real_part = jax.random.normal(first, (F, M, M), jnp.float32)
    imag_part = jax.random.normal(second, (F, M, M), jnp.float32)
    outer_rr = jnp.einsum('fik,fjk->fij', real_part, real_part, precision=lax.Precision.HIGHEST)
    outer_ii = jnp.einsum('fik,fjk->fij', imag_part, imag_part, precision=lax.Precision.HIGHEST)
    outer_ir = jnp.einsum('fik,fjk->fij', imag_part, real_part, precision=lax.Precision.HIGHEST)
    gram_real = (outer_rr + outer_ii) / M
    gram_imag = (outer_ir - jnp.swapaxes(outer_ir, 1, 2)) / M
    loading = jax.random.uniform(third, (F, M), jnp.float32, 1.0, 2.0)
    scales = jnp.exp(jax.random.uniform(fourth, (F, M), jnp.float32, 0.0, jnp.log(4.0)))
    gram_real = gram_real + jnp.eye(M, dtype=jnp.float32)[None] * loading[:, :, None]
    outer_scale = scales[:, :, None] * scales[:, None, :]
    return jnp.stack([gram_real * outer_scale, gram_imag * outer_scale], axis=1)


def draw_csm(key, part):
    return hermitian(jax.random.fold_in(key, 11)).astype(jnp.bfloat16)


def draw_inverse(key, part):
    return hermitian(jax.random.fold_in(key, 23)).astype(jnp.bfloat16)


def block_scale(key, dims, shards, least, high):
    level = 1.0
    for axis_at, blocks in shards:
        heights = jax.random.uniform(jax.random.fold_in(jax.random.fold_in(key, 6), axis_at), (blocks,), jnp.float32, least / len(shards), high / len(shards))
        level = level * jnp.repeat(jnp.exp(heights), dims[axis_at] // blocks).reshape((-1,) + (1,) * (len(dims) - 1 - axis_at))
    return level


def bell_draw(stream_key, shape, deviation, most, pieces=(), kind=jnp.bfloat16):
    drawn = jax.random.normal(stream_key, shape, jnp.float32) * deviation
    if len(pieces) > 0:
        drawn = block_scale(stream_key, shape, pieces, -0.22, 0.18) * drawn
    return jnp.clip(drawn, min=-most, max=most).astype(kind)


def setup_inputs(seed: int = 0) -> dict:
    splits = jax.random.split(jax.random.key(seed), 4)
    return {
        "replicas": bell_draw(splits[0], (F, G, 2, M), 1.0, 6.0, ((1, 32),)),
        "csm": draw_csm(jax.random.fold_in(splits[3], 71), 0),
        "inverse": draw_inverse(jax.random.fold_in(splits[3], 71), 0),
    }


def stacked(mat):
    real = mat[0].astype(jnp.float32)
    imag = mat[1].astype(jnp.float32)
    upper = jnp.concatenate([real, -imag], axis=1)
    lower = jnp.concatenate([imag, real], axis=1)
    return jnp.concatenate([upper, lower], axis=0)


def one_bin(inputs):
    vectors, matrix, inverted = inputs
    count = vectors.shape[0]
    wide = vectors.reshape(count, 2 * vectors.shape[2]).astype(jnp.float32)
    energy = jnp.sum(wide * wide, axis=1) + 1e-6
    power = jnp.sum(jnp.dot(wide, stacked(matrix), precision=lax.Precision.HIGHEST) * wide, axis=1)
    quad = jnp.sum(jnp.dot(wide, stacked(inverted), precision=lax.Precision.HIGHEST) * wide, axis=1)
    single_b = power / energy
    single_m = energy / quad
    return single_b / jnp.max(single_b), single_m / jnp.max(single_m)


def reference(replicas, csm, inverse):
    surf_b, surf_m = lax.map(one_bin, (replicas, csm, inverse))
    bins = replicas.shape[0]
    return jnp.sum(surf_b, axis=0) / bins, jnp.sum(surf_m, axis=0) / bins
```

```python
import functools

import jax
import jax.numpy as jnp
from jax import lax
from jax.experimental import pallas as pl
from jax.experimental.pallas import tpu as pltpu
from jax.sharding import PartitionSpec as P

GROUP = 8


def kernel(
    n, total_bins, rep_hbm, csm_ref, inv_ref, bart_ref, mvdr_ref,
    held, vecs, even, odd, mine, peaks, rep_sem, send_sem, recv_sem, out_sem, in_sem,
):
    bins, points, _, width = rep_hbm.shape
    rows = csm_ref.shape[2]
    half = width // 2
    far = n // GROUP
    me = lax.axis_index("grid")
    core = lax.rem(me, 2)
    low = lax.rem(me, GROUP)
    level = me // GROUP

    def flipped(index, bit):
        return index + bit * (1 - 2 * lax.rem(index // bit, 2))

    first = 2 + 2 * core
    second = 6 - first
    other = me + 1 - 2 * core
    across_a = flipped(me, first)
    across_b = flipped(me, second)
    stacked = [lax.rem(level + step, far) * GROUP + low for step in range(1, far)]

    barrier = pltpu.get_barrier_semaphore()
    for peer in [other, across_a, across_b] + stacked:
        pl.semaphore_signal(barrier, inc=1, device_id={"grid": peer})

    loads = []
    for f in range(bins):
        load = pltpu.make_async_copy(rep_hbm.at[f], vecs.at[f], rep_sem.at[f])
        load.start()
        loads.append(load)

    row_at = lax.broadcasted_iota(jnp.int32, (rows, width), 0) + me * rows
    col_at = lax.broadcasted_iota(jnp.int32, (rows, width), 1)
    upper = jnp.where(col_at > row_at, 1.0, jnp.where(col_at == row_at, 0.5, 0.0))
    lower = jnp.where(col_at < row_at, 1.0, 0.0)
    for m, ref in enumerate((csm_ref, inv_ref)):
        for f in range(bins):
            real = ref[f, 0].astype(jnp.float32)
            imag = ref[f, 1].astype(jnp.float32)
            held[m, me, f] = (real * upper + imag * lower).astype(jnp.bfloat16)

    pl.semaphore_wait(barrier, 2 + far)

    sends = []

    def send(m, owner, peer):
        k = len(sends)
        copy = pltpu.make_async_remote_copy(
            src_ref=held.at[m, owner],
            dst_ref=held.at[m, owner],
            send_sem=send_sem.at[k],
            recv_sem=recv_sem.at[m, owner],
            device_id={"grid": peer},
        )
        copy.start()
        sends.append(copy)

    def arrive(m, owner):
        pltpu.make_async_copy(held.at[m, owner], held.at[m, owner], recv_sem.at[m, owner]).wait()

    def split(f):
        loads[f].wait()
        block = min(points, 128)
        at = lax.broadcasted_iota(jnp.int32, (2 * block, 2 * block), 0)
        source = lax.broadcasted_iota(jnp.int32, (2 * block, 2 * block), 1)
        wanted = jnp.where(at < block, 2 * at, 2 * (at - block) + 1)
        pick = jnp.where(source == wanted, 1.0, 0.0).astype(jnp.bfloat16)

        def step(b, carry):
            where = pl.ds(pl.multiple_of(b * block, block), block)
            mixed = vecs[f, where].reshape(2 * block, width)
            apart = jnp.dot(pick, mixed, preferred_element_type=jnp.float32)
            re = apart[:block].astype(jnp.bfloat16)
            im = apart[block:].astype(jnp.bfloat16)
            for h in range(2):
                cols = slice(h * half, (h + 1) * half)
                even[f, where, 2 * h * half:(2 * h + 1) * half] = im[:, cols]
                even[f, where, (2 * h + 1) * half:(2 * h + 2) * half] = re[:, cols]
                odd[f, where, 2 * h * half:(2 * h + 1) * half] = -re[:, cols]
                odd[f, where, (2 * h + 1) * half:(2 * h + 2) * half] = im[:, cols]
            return carry

        lax.fori_loop(0, points // block, step, 0)

    lanes = 128
    ones = jnp.ones((8, lanes), jnp.float32)

    def fold(value):
        total = value[:, :lanes]
        for k in range(1, value.shape[1] // lanes):
            total = total + value[:, k * lanes:(k + 1) * lanes]
        return total

    def to_lanes(part):
        return lax.dot_general(
            ones, part, (((1,), (1,)), ((), ())),
            precision=lax.Precision.HIGHEST, preferred_element_type=jnp.float32,
        )[0:1]

    def energy_of(f):
        wide = even[f].astype(jnp.float32)
        return to_lanes(fold(wide * wide)) + 1e-06

    tri_row = lax.broadcasted_iota(jnp.int32, (half, half), 0)
    tri_col = lax.broadcasted_iota(jnp.int32, (half, half), 1)
    keep_up = jnp.where(tri_col >= tri_row, 1.0, 0.0).astype(jnp.bfloat16)
    keep_low = jnp.where(tri_col < tri_row, 1.0, 0.0).astype(jnp.bfloat16)

    def form(m, f):
        whole = held[m, :, f].reshape(width, width)
        p00, p01 = whole[:half, :half], whole[:half, half:]
        p10, p11 = whole[half:, :half], whole[half:, half:]
        left = jnp.concatenate([p00 * keep_low, p00 * keep_up, p10], axis=0)
        right = jnp.concatenate([p01, p11 * keep_low, p11 * keep_up], axis=0)
        outs = []
        step = min(points, 256)
        for b in range(points // step):
            where = slice(b * step, (b + 1) * step)
            total = None
            for ref, weigh in ((even, 1), (odd, 1)):
                for h, mat in enumerate((left, right)):
                    image = jnp.dot(
                        ref[f, where, h * half:h * half + 3 * half], mat,
                        preferred_element_type=jnp.float32,
                    )
                    match = ref[f, where, (2 * h + 1) * half:(2 * h + 2) * half]
                    term = fold(image * match.astype(jnp.float32))
                    total = term if total is None else total + term
            outs.append(to_lanes(total))
        return 2.0 * jnp.concatenate(outs, axis=1)

    owners_z = [lax.rem(level + far - step, far) * GROUP + low for step in range(1, far)]
    column = [me] + owners_z
    column_a = [flipped(o, first) for o in column]
    column_b = [flipped(o, second) for o in column]
    column_ab = [flipped(o, second) for o in column_a]

    for m in range(2):
        for peer in [across_a, across_b] + stacked + [other]:
            send(m, me, peer)

    split(0)
    for m in range(2):
        for owner in owners_z:
            arrive(m, owner)
            for peer in (across_a, across_b, other):
                send(m, owner, peer)
    for f in range(1, bins):
        split(f)
    energies = [energy_of(f) for f in range(bins)]
    for m in range(2):
        for owner in column_a:
            arrive(m, owner)
            send(m, owner, across_b)
            send(m, owner, other)

    def finish(m):
        for owner in column_b + column_ab:
            arrive(m, owner)
            send(m, owner, other)

    def partner(m):
        for owner in column + column_a + column_b + column_ab:
            arrive(m, owner + 1 - 2 * core)

    finish(0)
    partner(0)
    single = [form(0, f) / energies[f] for f in range(bins)]
    finish(1)
    partner(1)
    single += [energies[f] / form(1, f) for f in range(bins)]

    for k, value in enumerate(single):
        mine[k:k + 1] = jnp.broadcast_to(jnp.max(value, axis=1, keepdims=True), (1, lanes))

    shouts = []
    for step in range(1, n):
        copy = pltpu.make_async_remote_copy(
            src_ref=mine,
            dst_ref=peaks.at[step - 1],
            send_sem=out_sem.at[step - 1],
            recv_sem=in_sem.at[step - 1],
            device_id={"grid": lax.rem(me + step, n)},
        )
        copy.start()
        shouts.append(copy)
    for copy in sends:
        copy.wait_send()
    for copy in shouts:
        copy.wait_recv()
    top = jnp.maximum(jnp.max(peaks[...], axis=0), mine[...])
    for ref, at in ((bart_ref, 0), (mvdr_ref, bins)):
        total = None
        for f in range(bins):
            term = single[at + f] / top[at + f:at + f + 1, 0:1]
            total = term if total is None else total + term
        ref[...] = total / total_bins
    for copy in shouts:
        copy.wait_send()


def body(n, replicas, csm, inverse):
    bins, points, _, width = replicas.shape
    rows = csm.shape[2]
    over = lax.axis_size("freq")
    far = n // GROUP
    copies = 2 * (n - 1)
    vmem = pl.BlockSpec(memory_space=pltpu.VMEM)
    bart, mvdr = pl.pallas_call(
        functools.partial(kernel, n, bins * over),
        out_shape=[jax.ShapeDtypeStruct((1, points), jnp.float32)] * 2,
        in_specs=[pl.BlockSpec(memory_space=pl.ANY), vmem, vmem],
        out_specs=[vmem, vmem],
        scratch_shapes=[
            pltpu.VMEM((2, n, bins, rows, width), jnp.bfloat16),
            pltpu.VMEM((bins, points, 2, width), jnp.bfloat16),
            pltpu.VMEM((bins, points, 2 * width), jnp.bfloat16),
            pltpu.VMEM((bins, points, 2 * width), jnp.bfloat16),
            pltpu.VMEM((2 * bins, 128), jnp.float32),
            pltpu.VMEM((n - 1, 2 * bins, 128), jnp.float32),
            pltpu.SemaphoreType.DMA((bins,)),
            pltpu.SemaphoreType.DMA((copies,)),
            pltpu.SemaphoreType.DMA((2, n)),
            pltpu.SemaphoreType.DMA((n - 1,)),
            pltpu.SemaphoreType.DMA((n - 1,)),
        ],
        compiler_params=pltpu.CompilerParams(
            collective_id=0, has_side_effects=True, vmem_limit_bytes=48 * 1024 * 1024
        ),
    )(replicas, csm, inverse)
    if over == 1:
        return bart.reshape(points), mvdr.reshape(points)
    whole = lax.psum(jnp.concatenate([bart, mvdr], axis=0), "freq")
    share = points // over
    summed = lax.dynamic_slice_in_dim(whole, lax.axis_index("freq") * share, share, 1)
    return summed[0], summed[1]


def solution(mesh):
    in_specs = (
        P("freq", "grid", None, None),
        P("freq", None, "grid", None),
        P("freq", None, "grid", None),
    )
    out_specs = (P(("grid", "freq")), P(("grid", "freq")))
    return jax.shard_map(
        functools.partial(body, mesh.shape["grid"]),
        mesh=mesh, in_specs=in_specs, out_specs=out_specs, check_vma=False,
    )
```

```python
import functools

import jax
import jax.numpy as jnp
from jax import lax
from jax.experimental import pallas as pl
from jax.experimental.pallas import tpu as pltpu
from jax.sharding import PartitionSpec as P

GROUP = 8


def kernel(
    n, total_bins, rep_hbm, csm_hbm, inv_hbm, out_ref,
    held, vecs, slabs, even, odd, mine, peaks, rep_sem, slab_sem, send_sem, recv_sem, out_sem, in_sem,
):
    bins, points, _, width = rep_hbm.shape
    rows = csm_hbm.shape[2]
    half = width // 2
    far = n // GROUP
    me = lax.axis_index("grid")
    core = lax.rem(me, 2)
    low = lax.rem(me, GROUP)
    level = me // GROUP

    def flipped(index, bit):
        return index + bit * (1 - 2 * lax.rem(index // bit, 2))

    first = 2 + 2 * core
    second = 6 - first
    other = me + 1 - 2 * core
    across_a = flipped(me, first)
    across_b = flipped(me, second)
    stacked = [lax.rem(level + step, far) * GROUP + low for step in range(1, far)]

    pieces = []
    for m, ref in enumerate((csm_hbm, inv_hbm)):
        piece = pltpu.make_async_copy(ref, slabs.at[m], slab_sem.at[m])
        piece.start()
        pieces.append(piece)

    barrier = pltpu.get_barrier_semaphore()
    for peer in [other, across_a, across_b] + stacked:
        pl.semaphore_signal(barrier, inc=1, device_id={"grid": peer})

    loads = []
    for f in range(bins):
        load = pltpu.make_async_copy(rep_hbm.at[f], vecs.at[f], rep_sem.at[f])
        load.start()
        loads.append(load)

    row_at = lax.broadcasted_iota(jnp.int32, (rows, width), 0) + me * rows
    col_at = lax.broadcasted_iota(jnp.int32, (rows, width), 1)
    upper = jnp.where(col_at > row_at, 1.0, jnp.where(col_at == row_at, 0.5, 0.0))
    lower = jnp.where(col_at < row_at, 1.0, 0.0)
    for m in range(2):
        pieces[m].wait()
        for f in range(bins):
            real = slabs[m, f, 0].astype(jnp.float32)
            imag = slabs[m, f, 1].astype(jnp.float32)
            held[m, me, f] = (real * upper + imag * lower).astype(jnp.bfloat16)

    pl.semaphore_wait(barrier, 2 + far)

    sends = []

    def send(m, owner, peer):
        k = len(sends)
        copy = pltpu.make_async_remote_copy(
            src_ref=held.at[m, owner],
            dst_ref=held.at[m, owner],
            send_sem=send_sem.at[k],
            recv_sem=recv_sem.at[m, owner],
            device_id={"grid": peer},
        )
        copy.start()
        sends.append(copy)

    def arrive(m, owner):
        pltpu.make_async_copy(held.at[m, owner], held.at[m, owner], recv_sem.at[m, owner]).wait()

    def split(f):
        loads[f].wait()
        block = min(points, 128)
        at = lax.broadcasted_iota(jnp.int32, (2 * block, 2 * block), 0)
        source = lax.broadcasted_iota(jnp.int32, (2 * block, 2 * block), 1)
        wanted = jnp.where(at < block, 2 * at, 2 * (at - block) + 1)
        pick = jnp.where(source == wanted, 1.0, 0.0).astype(jnp.bfloat16)

        def step(b, carry):
            where = pl.ds(pl.multiple_of(b * block, block), block)
            mixed = vecs[f, where].reshape(2 * block, width)
            apart = jnp.dot(pick, mixed, preferred_element_type=jnp.float32)
            re = apart[:block].astype(jnp.bfloat16)
            im = apart[block:].astype(jnp.bfloat16)
            for h in range(2):
                cols = slice(h * half, (h + 1) * half)
                even[f, where, 2 * h * half:(2 * h + 1) * half] = im[:, cols]
                even[f, where, (2 * h + 1) * half:(2 * h + 2) * half] = re[:, cols]
                odd[f, where, 2 * h * half:(2 * h + 1) * half] = -re[:, cols]
                odd[f, where, (2 * h + 1) * half:(2 * h + 2) * half] = im[:, cols]
            return carry

        lax.fori_loop(0, points // block, step, 0)

    lanes = 128
    ones = jnp.ones((8, lanes), jnp.float32)

    def fold(value):
        total = value[:, :lanes]
        for k in range(1, value.shape[1] // lanes):
            total = total + value[:, k * lanes:(k + 1) * lanes]
        return total

    def to_lanes(part):
        return lax.dot_general(
            ones, part, (((1,), (1,)), ((), ())),
            precision=lax.Precision.HIGHEST, preferred_element_type=jnp.float32,
        )[0:1]

    def energy_of(f):
        wide = even[f].astype(jnp.float32)
        return to_lanes(fold(wide * wide)) + 1e-06

    tri_row = lax.broadcasted_iota(jnp.int32, (half, half), 0)
    tri_col = lax.broadcasted_iota(jnp.int32, (half, half), 1)
    keep_up = jnp.where(tri_col >= tri_row, 1.0, 0.0).astype(jnp.bfloat16)
    keep_low = jnp.where(tri_col < tri_row, 1.0, 0.0).astype(jnp.bfloat16)

    def form(m, f):
        whole = held[m, :, f].reshape(width, width)
        p00, p01 = whole[:half, :half], whole[:half, half:]
        p10, p11 = whole[half:, :half], whole[half:, half:]
        left = jnp.concatenate([p00 * keep_low, p00 * keep_up, p10], axis=0)
        right = jnp.concatenate([p01, p11 * keep_low, p11 * keep_up], axis=0)
        outs = []
        step = min(points, 512)
        for b in range(points // step):
            where = slice(b * step, (b + 1) * step)
            total = None
            for ref, weigh in ((even, 1), (odd, 1)):
                for h, mat in enumerate((left, right)):
                    image = jnp.dot(
                        ref[f, where, h * half:h * half + 3 * half], mat,
                        preferred_element_type=jnp.float32,
                    )
                    match = ref[f, where, (2 * h + 1) * half:(2 * h + 2) * half]
                    term = fold(image * match.astype(jnp.float32))
                    total = term if total is None else total + term
            outs.append(to_lanes(total))
        return 2.0 * jnp.concatenate(outs, axis=1)

    owners_z = [lax.rem(level + far - step, far) * GROUP + low for step in range(1, far)]
    column = [me] + owners_z
    column_a = [flipped(o, first) for o in column]
    column_b = [flipped(o, second) for o in column]
    column_ab = [flipped(o, second) for o in column_a]

    for m in range(2):
        for peer in [across_a, across_b] + stacked + [other]:
            send(m, me, peer)

    def pass_z(m):
        for owner in owners_z:
            arrive(m, owner)
            for peer in (across_b, across_a, other):
                send(m, owner, peer)

    def pass_a(m):
        for owner in column_a:
            arrive(m, owner)
            send(m, owner, across_b)
            send(m, owner, other)

    def pass_b(m, owners):
        for owner in owners:
            arrive(m, owner)
            send(m, owner, other)

    def partner(m):
        for owner in column + column_a + column_b + column_ab:
            arrive(m, owner + 1 - 2 * core)

    split(0)
    pass_z(0)
    for f in range(1, bins):
        split(f)
    energies = [energy_of(f) for f in range(bins)]
    pass_a(0)
    pass_z(1)
    pass_b(0, column_b + column_ab)
    pass_a(1)
    partner(0)
    single = [form(0, 0) / energies[0]]
    pass_b(1, column_b)
    single += [form(0, f) / energies[f] for f in range(1, bins)]
    pass_b(1, column_ab)
    partner(1)
    single += [energies[f] / form(1, f) for f in range(bins)]

    for k, value in enumerate(single):
        mine[k:k + 1] = jnp.broadcast_to(jnp.max(value, axis=1, keepdims=True), (1, lanes))

    shouts = []
    for step in range(1, n):
        copy = pltpu.make_async_remote_copy(
            src_ref=mine,
            dst_ref=peaks.at[step - 1],
            send_sem=out_sem.at[step - 1],
            recv_sem=in_sem.at[step - 1],
            device_id={"grid": lax.rem(me + step, n)},
        )
        copy.start()
        shouts.append(copy)
    for copy in sends:
        copy.wait_send()
    for copy in shouts:
        copy.wait_recv()
    top = jnp.maximum(jnp.max(peaks[...], axis=0), mine[...])
    for row in range(2):
        at = row * bins
        total = None
        for f in range(bins):
            term = single[at + f] / top[at + f:at + f + 1, 0:1]
            total = term if total is None else total + term
        out_ref[row:row + 1] = total / total_bins
    for copy in shouts:
        copy.wait_send()


def body(n, replicas, csm, inverse):
    bins, points, _, width = replicas.shape
    rows = csm.shape[2]
    over = lax.axis_size("freq")
    far = n // GROUP
    copies = 2 * (n - 1)
    whole = pl.pallas_call(
        functools.partial(kernel, n, bins * over),
        out_shape=jax.ShapeDtypeStruct((2, points), jnp.float32),
        in_specs=[pl.BlockSpec(memory_space=pltpu.HBM)] * 3,
        out_specs=pl.BlockSpec(memory_space=pltpu.VMEM),
        scratch_shapes=[
            pltpu.VMEM((2, n, bins, rows, width), jnp.bfloat16),
            pltpu.VMEM((bins, points, 2, width), jnp.bfloat16),
            pltpu.VMEM((2, bins, 2, rows, width), jnp.bfloat16),
            pltpu.VMEM((bins, points, 2 * width), jnp.bfloat16),
            pltpu.VMEM((bins, points, 2 * width), jnp.bfloat16),
            pltpu.VMEM((2 * bins, 128), jnp.float32),
            pltpu.VMEM((n - 1, 2 * bins, 128), jnp.float32),
            pltpu.SemaphoreType.DMA((bins,)),
            pltpu.SemaphoreType.DMA((2,)),
            pltpu.SemaphoreType.DMA((copies,)),
            pltpu.SemaphoreType.DMA((2, n)),
            pltpu.SemaphoreType.DMA((n - 1,)),
            pltpu.SemaphoreType.DMA((n - 1,)),
        ],
        compiler_params=pltpu.CompilerParams(
            collective_id=0, has_side_effects=True, vmem_limit_bytes=67043328
        ),
    )(replicas, csm, inverse)
    if over == 1:
        return whole[0], whole[1]
    whole = lax.psum(whole, "freq")
    share = points // over
    summed = lax.dynamic_slice_in_dim(whole, lax.axis_index("freq") * share, share, 1)
    return summed[0], summed[1]


def solution(mesh):
    in_specs = (
        P("freq", "grid", None, None),
        P("freq", None, "grid", None),
        P("freq", None, "grid", None),
    )
    out_specs = (P(("grid", "freq")), P(("grid", "freq")))
    return jax.shard_map(
        functools.partial(body, mesh.shape["grid"]),
        mesh=mesh, in_specs=in_specs, out_specs=out_specs, check_vma=False,
    )
```

```python
import functools

import jax
import jax.numpy as jnp
from jax import lax
from jax.experimental import pallas as pl
from jax.experimental.pallas import tpu as pltpu
from jax.sharding import PartitionSpec as P

GROUP = 8


def kernel(
    n, total_bins, rep_hbm, csm_hbm, inv_hbm, out_ref,
    held, vecs, slabs, natural, even, odd, ups, lows, parts, mine, peaks, rep_sem, slab_sem, send_sem, recv_sem, out_sem, in_sem,
):
    bins, points, _, width = rep_hbm.shape
    rows = csm_hbm.shape[2]
    wide = width // 4
    far = n // GROUP
    me = lax.axis_index("grid")
    core = lax.rem(me, 2)
    low = lax.rem(me, GROUP)
    level = me // GROUP

    def flipped(index, bit):
        return index + bit * (1 - 2 * lax.rem(index // bit, 2))

    first = 2 + 2 * core
    second = 6 - first
    other = me + 1 - 2 * core
    across_a = flipped(me, first)
    across_b = flipped(me, second)
    stacked = [lax.rem(level + step, far) * GROUP + low for step in range(1, far)]

    pieces = []
    for m, ref in enumerate((csm_hbm, inv_hbm)):
        piece = pltpu.make_async_copy(ref, slabs.at[m], slab_sem.at[m])
        piece.start()
        pieces.append(piece)

    barrier = pltpu.get_barrier_semaphore()
    for peer in [other, across_a, across_b] + stacked:
        pl.semaphore_signal(barrier, inc=1, device_id={"grid": peer})

    loads = []
    for f in range(bins):
        load = pltpu.make_async_copy(rep_hbm.at[f], vecs.at[f], rep_sem.at[f])
        load.start()
        loads.append(load)

    row_at = lax.broadcasted_iota(jnp.int32, (rows, width), 0) + me * rows
    col_at = lax.broadcasted_iota(jnp.int32, (rows, width), 1)
    upper = jnp.where(col_at > row_at, 1.0, jnp.where(col_at == row_at, 0.5, 0.0))
    lower = jnp.where(col_at < row_at, 1.0, 0.0)
    for m in range(2):
        pieces[m].wait()
        for f in range(bins):
            real = slabs[m, f, 0].astype(jnp.float32)
            imag = slabs[m, f, 1].astype(jnp.float32)
            held[m * bins + f, me] = (real * upper + imag * lower).astype(jnp.bfloat16)

    pl.semaphore_wait(barrier, 2 + far)

    sends = []

    def send(m, owner, peer):
        k = len(sends)
        copy = pltpu.make_async_remote_copy(
            src_ref=held.at[m, owner],
            dst_ref=held.at[m, owner],
            send_sem=send_sem.at[k],
            recv_sem=recv_sem.at[m, owner],
            device_id={"grid": peer},
        )
        copy.start()
        sends.append(copy)

    def arrive(m, owner):
        pltpu.make_async_copy(held.at[m, owner], held.at[m, owner], recv_sem.at[m, owner]).wait()

    owners_z = [lax.rem(level + far - step, far) * GROUP + low for step in range(1, far)]
    column = [me] + owners_z
    column_a = [flipped(o, first) for o in column]
    column_b = [flipped(o, second) for o in column]
    column_ab = [flipped(o, second) for o in column_a]
    across = [[o + 1 - 2 * core for o in part] for part in (column, column_b, column_a, column_ab)]
    groups = [
        column + across[0], column_a + across[1], column_b + across[2], column_ab + across[3]
    ]
    order = [owner for group in groups for owner in group]

    def element(shape, axis):
        at = lax.broadcasted_iota(jnp.int32, shape, axis)
        inside = lax.rem(at, rows)
        found = inside
        for k, owner in enumerate(order):
            found = jnp.where((at >= k * rows) & (at < (k + 1) * rows), owner * rows + inside, found)
        return found

    def split(f):
        loads[f].wait()
        block = min(points, 128)
        at = lax.broadcasted_iota(jnp.int32, (2 * block, 2 * block), 0)
        source = lax.broadcasted_iota(jnp.int32, (2 * block, 2 * block), 1)
        wanted = jnp.where(at < block, 2 * at, 2 * (at - block) + 1)
        pick = jnp.where(source == wanted, 1.0, 0.0).astype(jnp.bfloat16)

        def step(b, carry):
            where = pl.ds(pl.multiple_of(b * block, block), block)
            mixed = vecs[f, where].reshape(2 * block, width)
            apart = jnp.dot(pick, mixed, preferred_element_type=jnp.float32)
            re = apart[:block].astype(jnp.bfloat16)
            im = apart[block:].astype(jnp.bfloat16)
            natural[f, 0, where] = re
            natural[f, 1, where] = im
            re = jnp.dot(re, moved, preferred_element_type=jnp.float32).astype(jnp.bfloat16)
            im = jnp.dot(im, moved, preferred_element_type=jnp.float32).astype(jnp.bfloat16)
            for g in range(4):
                cols = slice(g * wide, (g + 1) * wide)
                even[f, where, 2 * g * wide:(2 * g + 1) * wide] = re[:, cols]
                even[f, where, (2 * g + 1) * wide:(2 * g + 2) * wide] = im[:, cols]
                odd[f, where, 2 * g * wide:(2 * g + 1) * wide] = im[:, cols]
                odd[f, where, (2 * g + 1) * wide:(2 * g + 2) * wide] = -re[:, cols]
            return carry

        lax.fori_loop(0, points // block, step, 0)

    lanes = 128
    ones = jnp.ones((8, lanes), jnp.float32)

    def fold(value):
        total = value[:, :lanes]
        for k in range(1, value.shape[1] // lanes):
            total = total + value[:, k * lanes:(k + 1) * lanes]
        return total

    def to_lanes(part):
        return lax.dot_general(
            ones, part, (((1,), (1,)), ((), ())),
            precision=lax.Precision.HIGHEST, preferred_element_type=jnp.float32,
        )[0:1]

    def energy_of(f):
        re = natural[f, 0].astype(jnp.float32)
        im = natural[f, 1].astype(jnp.float32)
        return to_lanes(fold(re * re) + fold(im * im)) + 1e-06

    def work(m, g):
        f = m % bins
        block = jnp.concatenate([held[m, owner] for owner in groups[g]], axis=0)
        cols = slice(g * wide, (g + 1) * wide)
        mat = jnp.concatenate([block * ups[cols], block * lows[cols]], axis=0)
        total = None
        for ref, k in ((even, 0), (odd, 1)):
            image = jnp.dot(
                ref[f, :, 2 * g * wide:(2 * g + 2) * wide], mat, preferred_element_type=jnp.float32
            )
            term = fold(image * natural[f, k].astype(jnp.float32))
            total = term if total is None else total + term
        parts[m] = total if g == 0 else parts[m] + total

    phases = range(2 * bins)
    for m in phases:
        for peer in [across_b, across_a] + stacked + [other]:
            send(m, me, peer)

    def pass_z(m):
        for owner in owners_z:
            arrive(m, owner)
            for peer in (across_b, across_a, other):
                send(m, owner, peer)

    def pass_a(m):
        for owner in column_a:
            arrive(m, owner)
            send(m, owner, across_b)
            send(m, owner, other)

    def pass_b(m, owners):
        for owner in owners:
            arrive(m, owner)
            send(m, owner, other)

    def partner(m, g):
        for owner in across[g]:
            arrive(m, owner)

    spot = element((8, width), 1)[0:1]
    moved = jnp.where(
        lax.broadcasted_iota(jnp.int32, (width, width), 0) == spot, 1.0, 0.0
    ).astype(jnp.bfloat16)
    split(0)
    for m in phases:
        pass_z(m)
    for f in range(1, bins):
        split(f)
    rank = element((width, 128), 0)
    for k in range(width // 128):
        cols = slice(k * 128, (k + 1) * 128)
        lane = lax.broadcasted_iota(jnp.int32, (width, 128), 1) + k * 128
        ups[:, cols] = jnp.where(lane >= rank, 1.0, 0.0).astype(jnp.bfloat16)
        lows[:, cols] = jnp.where(lane < rank, 1.0, 0.0).astype(jnp.bfloat16)
    for m in phases:
        pass_a(m)
        pass_b(m, column_b)
    energies = [energy_of(f) for f in range(bins)]
    for m in phases:
        partner(m, 0)
        work(m, 0)
    for m in phases:
        pass_b(m, column_ab)
        partner(m, 1)
        work(m, 1)
        partner(m, 2)
        work(m, 2)
    single = []
    for m in phases:
        partner(m, 3)
        work(m, 3)
        form = 2.0 * to_lanes(parts[m])
        if m < bins:
            single.append(form / energies[m % bins])
        else:
            single.append(energies[m % bins] / form)

    for k, value in enumerate(single):
        mine[k:k + 1] = jnp.broadcast_to(jnp.max(value, axis=1, keepdims=True), (1, lanes))

    shouts = []
    for step in range(1, n):
        copy = pltpu.make_async_remote_copy(
            src_ref=mine,
            dst_ref=peaks.at[step - 1],
            send_sem=out_sem.at[step - 1],
            recv_sem=in_sem.at[step - 1],
            device_id={"grid": lax.rem(me + step, n)},
        )
        copy.start()
        shouts.append(copy)
    for copy in sends:
        copy.wait_send()
    for copy in shouts:
        copy.wait_recv()
    top = jnp.maximum(jnp.max(peaks[...], axis=0), mine[...])
    for row in range(2):
        at = row * bins
        total = None
        for f in range(bins):
            term = single[at + f] / top[at + f:at + f + 1, 0:1]
            total = term if total is None else total + term
        out_ref[row:row + 1] = total / total_bins
    for copy in shouts:
        copy.wait_send()


def body(n, replicas, csm, inverse):
    bins, points, _, width = replicas.shape
    rows = csm.shape[2]
    over = lax.axis_size("freq")
    far = n // GROUP
    copies = 2 * bins * (n - 1)
    whole = pl.pallas_call(
        functools.partial(kernel, n, bins * over),
        out_shape=jax.ShapeDtypeStruct((2, points), jnp.float32),
        in_specs=[pl.BlockSpec(memory_space=pltpu.HBM)] * 3,
        out_specs=pl.BlockSpec(memory_space=pltpu.VMEM),
        scratch_shapes=[
            pltpu.VMEM((2 * bins, n, rows, width), jnp.bfloat16),
            pltpu.VMEM((bins, points, 2, width), jnp.bfloat16),
            pltpu.VMEM((2, bins, 2, rows, width), jnp.bfloat16),
            pltpu.VMEM((bins, 2, points, width), jnp.bfloat16),
            pltpu.VMEM((bins, points, 2 * width), jnp.bfloat16),
            pltpu.VMEM((bins, points, 2 * width), jnp.bfloat16),
            pltpu.VMEM((width, width), jnp.bfloat16),
            pltpu.VMEM((width, width), jnp.bfloat16),
            pltpu.VMEM((2 * bins, points, 128), jnp.float32),
            pltpu.VMEM((2 * bins, 128), jnp.float32),
            pltpu.VMEM((n - 1, 2 * bins, 128), jnp.float32),
            pltpu.SemaphoreType.DMA((bins,)),
            pltpu.SemaphoreType.DMA((2,)),
            pltpu.SemaphoreType.DMA((copies,)),
            pltpu.SemaphoreType.DMA((2 * bins, n)),
            pltpu.SemaphoreType.DMA((n - 1,)),
            pltpu.SemaphoreType.DMA((n - 1,)),
        ],
        compiler_params=pltpu.CompilerParams(
            collective_id=0, has_side_effects=True, vmem_limit_bytes=67043328
        ),
    )(replicas, csm, inverse)
    if over == 1:
        return whole[0], whole[1]
    whole = lax.psum(whole, "freq")
    share = points // over
    summed = lax.dynamic_slice_in_dim(whole, lax.axis_index("freq") * share, share, 1)
    return summed[0], summed[1]


def solution(mesh):
    in_specs = (
        P("freq", "grid", None, None),
        P("freq", None, "grid", None),
        P("freq", None, "grid", None),
    )
    out_specs = (P(("grid", "freq")), P(("grid", "freq")))
    return jax.shard_map(
        functools.partial(body, mesh.shape["grid"]),
        mesh=mesh, in_specs=in_specs, out_specs=out_specs, check_vma=False,
    )
```
